32 devices in a mesh: groups: 2 (over y), sky: 16 (over z, x, core).
Axes of the slice: x: 2, y: 2, z: 4, core: 2. Of those that a mesh axis runs over, the one named last changes fastest.
Arguments:
- model: float32 [64, 6, 256, 128], P(('groups', 'sky')), parts along dimension 0, may hold values from 0 to 2
- exposures: bfloat16 [4096, 16, 128], P(('groups', 'sky')), parts along dimension 0, may hold values from -6 to 6
- inv_var: float32 [4096], P(('groups', 'sky')), parts along dimension 0, may hold values from 0.5 to 2
- step_size: float32 [6], replicated, may hold values from 0.2 to 0.6
- psf_taps: float32 [64, 56], P(('groups', 'sky')), parts along dimension 0, may hold values from 0.05 to 1
- exp_batch: int32 [4096], P(('groups', 'sky')), parts along dimension 0, may hold values from 0 to 31
- send_plane: int32 [512, 16], P(('groups', 'sky')), parts along dimension 0, may hold values from -1 to 11, as said below
- send_row: int32 [512, 16], P(('groups', 'sky')), parts along dimension 0, may hold values from 0 to 248, as said below
- send_cover: int32 [512, 16], P(('groups', 'sky')), parts along dimension 0, may hold values from 0 to 16, as said below
- use_slot: int32 [4096, 2], P(('groups', 'sky')), parts along dimension 0, may hold values from -1 to 255, as said below
- use_start: int32 [4096, 2], P(('groups', 'sky')), parts along dimension 0, may hold values from 0 to 8, as said below
- use_stop: int32 [4096, 2], P(('groups', 'sky')), parts along dimension 0, may hold values from 0 to 16
- foot_lo: int32 [64], P(('groups', 'sky')), parts along dimension 0, may hold values from 0 to 63
- foot_hi: int32 [64], P(('groups', 'sky')), parts along dimension 0, may hold values from 193 to 256
Outputs:
- updated_model: float32 [64, 6, 256, 128], P(('groups', 'sky')), parts along dimension 0
- residual: float32 [4096, 16, 128], P(('groups', 'sky')), parts along dimension 0
The draws below stay inside these ranges and needn't reach their ends.
There are 2 independent parts, one for each index of `groups`. The reference program is written for one: setup_inputs(seed, part) draws one part's arguments, and reference() takes and returns one part's arrays. A program takes and returns all parts, laid end to end along the dimension named above; an argument that names none is the same for every part. Nothing has to cross between parts.
Inputs may be any that keep to these rules, and one draw needn't show every extreme that they name: In each row of send_plane the covered rows of the live slots (send_cover) sum to at most 128, and on every device some row reaches it. A live slot of exposure owner d is used by exactly one intersection of one exposure on d, and every intersection with use_slot >= 0 names a live slot; all pieces of an exposure come from planes of one band. `send_row`: for a live slot, the tile rows that its piece covers lie inside the tile. send_cover of a live slot equals use_stop - use_start of the intersection that uses it. `use_slot`: each exposure has 1 to 2 live intersections, first in order; -1 after them. `use_start`: the live intersections of an exposure cover rows 0 to 15 in order without gaps; dead ones have start and stop 0.
All inputs are finite; a program needn't handle non-finite values.
Results may differ from the reference program's by a relative error of at most 0.0011.
Values may be sent and summed in bfloat16 or wider, within the bound.
A program may use at most 128 MiB of HBM per device.

```python
import math
import jax
import jax.numpy as jnp
from jax import lax

B = 6
W = 128
TR = 256
H = 16
TILE_DEV = 2
EXP_DEV = 128
K = 2
NPSF = 4
TAPS = 7
ITERS = 2
NT = 32
NE = 2048
NBATCH = 32
CAP = 16
N_SKY = 16


def routing(key):
    base = jax.random.fold_in(key, 7919)
    keys = jax.random.split(base, 5)
    half = H // 2
    budget = CAP * H // 2
    count = jax.random.randint(keys[0], (N_SKY, EXP_DEV), 1, 3)
    count = count.at[:, 0].set(1)
    band_of = jax.random.randint(keys[1], (N_SKY, EXP_DEV), 0, B)
    source_order = jax.vmap(lambda subkey: jax.random.permutation(subkey, N_SKY))(jax.random.split(keys[2], N_SKY))
    tile_of = jax.random.randint(keys[3], (N_SKY, EXP_DEV, K), 0, TILE_DEV)
    raw_offset = jax.random.randint(keys[4], (N_SKY, EXP_DEV, K), 0, 1 << 20)
    intersection = jnp.arange(K, dtype=jnp.int32)[None, None, :]
    alive = intersection < count[:, :, None]
    split_two = count[:, :, None] == 2
    start = jnp.where(alive & (intersection == 1), half, 0)
    length = jnp.where(alive, jnp.where(split_two, jnp.where(intersection == 0, half, H - half), H), 0)
    stop = jnp.where(alive, start + length, 0)
    position = jnp.arange(EXP_DEV, dtype=jnp.int32)[None, :, None] * H + start
    source_rank = position // budget
    slot_column = position % budget // half
    source = jnp.take_along_axis(source_order, source_rank.reshape(N_SKY, -1), axis=1).reshape(N_SKY, EXP_DEV, K)
    slot = source * CAP + slot_column
    tile_row = raw_offset % (TR - length + 1)
    plane = tile_of * B + band_of[:, :, None]
    slot_alive = jnp.where(alive, slot, -1)
    target = jnp.where(alive, slot, N_SKY * CAP).reshape(N_SKY, -1)
    owners = jnp.arange(N_SKY, dtype=jnp.int32)[:, None]
    table_plane = jnp.full((N_SKY, N_SKY * CAP), -1, jnp.int32).at[owners, target].set(plane.reshape(N_SKY, -1), mode='drop')
    table_row = jnp.zeros((N_SKY, N_SKY * CAP), jnp.int32).at[owners, target].set(tile_row.reshape(N_SKY, -1), mode='drop')
    table_cover = jnp.zeros((N_SKY, N_SKY * CAP), jnp.int32).at[owners, target].set(length.reshape(N_SKY, -1), mode='drop')
    send_plane = table_plane.reshape(N_SKY, N_SKY, CAP).transpose(1, 0, 2).reshape(N_SKY * N_SKY, CAP)
    send_row = table_row.reshape(N_SKY, N_SKY, CAP).transpose(1, 0, 2).reshape(N_SKY * N_SKY, CAP)
    send_cover = table_cover.reshape(N_SKY, N_SKY, CAP).transpose(1, 0, 2).reshape(N_SKY * N_SKY, CAP)
    return (slot_alive.reshape(NE, K).astype(jnp.int32), start.reshape(NE, K).astype(jnp.int32), stop.reshape(NE, K).astype(jnp.int32), send_plane.astype(jnp.int32), send_row.astype(jnp.int32), send_cover.astype(jnp.int32))


def draw_use_slot(key, part):
    return routing(key)[0]


def draw_use_start(key, part):
    return routing(key)[1]


def draw_use_stop(key, part):
    return routing(key)[2]


def draw_send_plane(key, part):
    return routing(key)[3]


def draw_send_row(key, part):
    return routing(key)[4]


def draw_send_cover(key, part):
    return routing(key)[5]


def place_ends(drawn, stream_key, low, high):
    dims = drawn.shape
    place = [jax.random.randint(jax.random.fold_in(stream_key, axis), (), 0, dims[axis]) for axis in range(len(dims))]
    drawn = drawn.at[tuple(place)].set(low)
    longest = dims.index(max(dims))
    place[longest] = (place[longest] + 1) % dims[longest]
    return drawn.at[tuple(place)].set(high)


def levels(key, shape, cuts, low, top_value):
    def one(axis_at, shards_of):
        draws = jax.random.uniform(jax.random.fold_in(jax.random.fold_in(key, 6), axis_at), (shards_of,), jnp.float32, low / len(cuts), top_value / len(cuts))
        return jnp.repeat(jnp.exp(draws), shape[axis_at] // shards_of).reshape((-1,) + (1,) * (len(shape) - axis_at - 1))

    loudness = one(*cuts[0])
    for cut in cuts[1:]:
        loudness = loudness * one(*cut)
    return loudness


def noise(stream_key, shape, width, most, cuts=(), kind=jnp.bfloat16):
    array = jax.random.normal(stream_key, shape, jnp.float32) * width
    if len(cuts) > 0:
        array = levels(stream_key, shape, cuts, -0.22, 0.18) * array
    return jnp.clip(array, min=-most, max=most).astype(kind)


def setup_inputs(seed: int = 0, part: int = 0) -> dict:
    splits = jax.random.split(jax.random.key(seed), 15)
    part_keys = jax.random.split(jax.random.fold_in(splits[14], part), 15)
    return {
        "model": jnp.clip(2.0 * jax.random.uniform(part_keys[0], (NT, B, TR, W), jnp.float32) ** levels(part_keys[0], (NT, B, TR, W), ((0, 16),), -0.2, 0.2), 0.0, 2.0),
        "exposures": noise(part_keys[1], (NE, H, W), 1.0, 6.0, ((0, 16),)),
        "inv_var": jnp.clip(jnp.exp(math.log(2.0) - 1.3862944 * jax.random.uniform(part_keys[2], (NE,), jnp.float32) ** levels(part_keys[2], (NE,), ((0, 16),), -0.2, 0.2)), 0.5, 2.0),
        "step_size": jnp.clip(jnp.exp(jax.random.uniform(splits[3], (B,), jnp.float32, math.log(0.2), math.log(0.6))), 0.2, 0.6),
        "psf_taps": jnp.clip(0.05 + 0.95 * jax.random.uniform(part_keys[4], (NBATCH, 2 * NPSF * TAPS), jnp.float32) ** levels(part_keys[4], (NBATCH, 2 * NPSF * TAPS), ((0, 16),), -0.2, 0.2), 0.05, 1.0),
        "exp_batch": place_ends(jax.random.randint(part_keys[5], (NE,), 0, NBATCH), jax.random.fold_in(part_keys[5], 1), 0, NBATCH - 1).astype(jnp.int32),
        "send_plane": draw_send_plane(jax.random.fold_in(jax.random.fold_in(splits[14], part), 71), part),
        "send_row": draw_send_row(jax.random.fold_in(jax.random.fold_in(splits[14], part), 71), part),
        "send_cover": draw_send_cover(jax.random.fold_in(jax.random.fold_in(splits[14], part), 71), part),
        "use_slot": draw_use_slot(jax.random.fold_in(jax.random.fold_in(splits[14], part), 71), part),
        "use_start": draw_use_start(jax.random.fold_in(jax.random.fold_in(splits[14], part), 71), part),
        "use_stop": draw_use_stop(jax.random.fold_in(jax.random.fold_in(splits[14], part), 71), part),
        "foot_lo": place_ends(jax.random.randint(part_keys[12], (NT,), 0, TR // 4), jax.random.fold_in(part_keys[12], 1), 0, (TR // 4) - 1).astype(jnp.int32),
        "foot_hi": place_ends(jax.random.randint(part_keys[13], (NT,), TR - TR // 4 + 1, TR + 1), jax.random.fold_in(part_keys[13], 1), TR - TR // 4 + 1, TR).astype(jnp.int32),
    }


def build_ops(kernel_taps, extent):
    half_width = kernel_taps.shape[-1] // 2
    offset_grid = lax.broadcasted_iota(jnp.int32, (extent, extent), 0) - lax.broadcasted_iota(jnp.int32, (extent, extent), 1) + half_width
    onehot = (offset_grid[:, :, None] == jnp.arange(kernel_taps.shape[-1], dtype=jnp.int32)[None, None, :]).astype(jnp.float32)
    return jnp.einsum("ejt,abt->ejab", kernel_taps, onehot, precision=lax.Precision.HIGHEST).astype(jnp.bfloat16)


def block_step(padded, exposures, inv_var, taps_rows, use_slot, use_start, use_stop, send_plane, send_row, send_cover, owner):
    f32 = jnp.float32
    kernel_taps = taps_rows.reshape(taps_rows.shape[0], 2, NPSF, TAPS)
    kernel_taps = kernel_taps / jnp.sum(kernel_taps, axis=-1, keepdims=True)
    row_ops = build_ops(kernel_taps[:, 0], H)
    col_ops = build_ops(kernel_taps[:, 1], W)
    alive = use_slot >= 0
    slot_safe = jnp.maximum(use_slot, 0)
    source = slot_safe // CAP
    column = slot_safe % CAP
    table_row = source * N_SKY + owner
    plane = send_plane[table_row, column]
    cover = send_cover[table_row, column]
    row_first = send_row[table_row, column] + H - use_start
    global_plane = source * (TILE_DEV * B) + jnp.maximum(plane, 0)

    def take_piece(plane_id, row_start):
        return lax.dynamic_slice(padded, (plane_id, row_start, jnp.int32(0)), (1, H, W))[0]

    pieces = jax.vmap(jax.vmap(take_piece))(global_plane, row_first)
    row_pos = jnp.arange(H, dtype=jnp.int32)
    ahead = row_pos[None, None, :] >= use_start[:, :, None]
    forward = ahead & (row_pos[None, None, :] < use_start[:, :, None] + cover[:, :, None]) & alive[:, :, None]
    covered = ahead & (row_pos[None, None, :] < use_stop[:, :, None]) & alive[:, :, None]
    stamps = jnp.sum(jnp.where(forward[..., None], pieces.astype(f32), 0.0), axis=1).astype(jnp.bfloat16)
    blurred = jnp.einsum("erd,ejcd->erjc", stamps.astype(f32), col_ops.astype(f32)).astype(jnp.bfloat16)
    predicted = jnp.einsum("ejrs,esjc->erc", row_ops.astype(f32), blurred.astype(f32)) / NPSF
    residual = inv_var[:, None, None] * (predicted - exposures.astype(f32))
    back = jnp.einsum("ejsr,esc->erjc", row_ops.astype(f32), residual.astype(jnp.bfloat16).astype(f32)).astype(jnp.bfloat16)
    correlated = (jnp.einsum("erjc,ejcd->erd", back.astype(f32), col_ops.astype(f32)) / NPSF).astype(jnp.bfloat16)
    contrib = jnp.where(covered[..., None], correlated[:, None].astype(f32), 0.0)
    target = jnp.where(alive, global_plane, NT * B)
    return residual, target, row_first, contrib


def reference(model, exposures, inv_var, step_size, psf_taps, exp_batch, send_plane, send_row, send_cover, use_slot, use_start, use_stop, foot_lo, foot_hi):
    taps_all = psf_taps[exp_batch]
    current = model
    row_pos = jnp.arange(H, dtype=jnp.int32)
    tile_pos = jnp.arange(TR, dtype=jnp.int32)
    inside = (tile_pos[None, :] >= foot_lo[:, None]) & (tile_pos[None, :] < foot_hi[:, None])
    residual_all = None
    for sweep in range(ITERS):
        planes = current.astype(jnp.bfloat16).reshape(NT * B, TR, W)
        padded = jnp.pad(planes, ((0, 0), (H, H), (0, 0)))

        def one_block(gradient, owner):
            first = owner * EXP_DEV
            residual, target, row_first, contrib = block_step(
                padded,
                lax.dynamic_slice_in_dim(exposures, first, EXP_DEV, 0),
                lax.dynamic_slice_in_dim(inv_var, first, EXP_DEV, 0),
                lax.dynamic_slice_in_dim(taps_all, first, EXP_DEV, 0),
                lax.dynamic_slice_in_dim(use_slot, first, EXP_DEV, 0),
                lax.dynamic_slice_in_dim(use_start, first, EXP_DEV, 0),
                lax.dynamic_slice_in_dim(use_stop, first, EXP_DEV, 0),
                send_plane, send_row, send_cover, owner)
            gradient = gradient.at[target[:, :, None], row_first[:, :, None] + row_pos[None, None, :]].add(contrib, mode="drop")
            return gradient, residual

        gradient, residual_all = lax.scan(one_block, jnp.zeros((NT * B, TR + 2 * H, W), jnp.float32), jnp.arange(N_SKY, dtype=jnp.int32))
        gradient = gradient[:, H:H + TR].reshape(NT, B, TR, W)
        updated = jnp.maximum(current - step_size[None, :, None, None] * gradient, 0.0)
        current = jnp.where(inside[:, None, :, None], updated, 0.0)
    return current, residual_all.reshape(NE, H, W)
```

```python
import functools

import jax
import jax.numpy as jnp
from jax import lax
from jax.experimental import pallas as pl
from jax.experimental.pallas import tpu as pltpu
from jax.sharding import PartitionSpec as P

NPSF = 4
TAPS = 7
ITERS = 2
F32 = jnp.float32
BF16 = jnp.bfloat16
I32 = jnp.int32


def vmem():
    return pl.BlockSpec(memory_space=pltpu.VMEM)


def hbm():
    return pl.BlockSpec(memory_space=pltpu.HBM)


def round_up(value, multiple):
    return -(-value // multiple) * multiple


def partner(me, i, peers):
    other = 0
    bit = 1
    while bit < peers:
        other = other + lax.rem(lax.div(me, bit) + lax.div(i, bit), 2) * bit
        bit *= 2
    return other


def iota(shape, axis):
    return lax.broadcasted_iota(I32, shape, axis)


def floor_div(value, divisor):
    return jnp.floor((value.astype(F32) + 0.5) * (1.0 / divisor))


def send_table(plane, row, cover, width, tile_rows):
    peers, capacity = plane.shape
    position = iota((peers, width), 1)
    chosen = jnp.zeros((peers, width), I32)
    offset = jnp.zeros((peers, 1), I32)
    for c in range(capacity):
        first = jnp.maximum(plane[:, c : c + 1], 0) * tile_rows + row[:, c : c + 1] - offset
        chosen = jnp.where(position >= offset, first + position, chosen)
        offset = offset + cover[:, c : c + 1]
    return chosen, position < offset


def use_tables(slot, start, stop, peers, capacity, rows_each, width, height):
    meets, count = slot.shape
    which_peer = iota((peers, count), 0).astype(F32)
    exposure = iota((1, count), 1).astype(F32)
    owners, columns, starts, lengths, alive, peer_rows = [], [], [], [], [], []
    for k in range(meets):
        name = slot[k : k + 1, :].astype(F32)
        peer = floor_div(name, capacity)
        owners.append(jnp.where(which_peer == peer, 1.0, 0.0))
        columns.append(name - peer * capacity)
        starts.append(start[k : k + 1, :].astype(F32))
        lengths.append(stop[k : k + 1, :].astype(F32) - starts[k])
        alive.append(name >= 0.0)
        peer_rows.append(peer)
    begin = jnp.zeros((peers, 1), F32)
    found = [jnp.zeros((1, count), F32) for _ in range(meets)]
    position = iota((peers, width), 1).astype(F32)
    chosen = jnp.zeros((peers, width), F32)
    for c in range(capacity):
        length = jnp.zeros((peers, count), F32)
        source = jnp.zeros((peers, count), F32)
        for k in range(meets):
            here = jnp.where(columns[k] == c, owners[k], 0.0)
            length = length + here * lengths[k]
            source = source + here * (exposure * height + starts[k])
            found[k] = found[k] + jnp.sum(here * begin, axis=0, keepdims=True)
        source = jnp.sum(source, axis=1, keepdims=True)
        chosen = jnp.where(position >= begin, source - begin + position, chosen)
        begin = begin + jnp.sum(length, axis=1, keepdims=True)
    give = jnp.clip(chosen.astype(I32), 0, count * height - 1)
    rows = []
    for k in range(meets):
        where = height + peer_rows[k] * rows_each + found[k] - starts[k]
        rows.append(jnp.where(alive[k], where, float(height)))
    for k in range(meets):
        rows.append(jnp.where(alive[k], starts[k], float(height)))
    limits = [peers * rows_each + height] * meets + [height] * meets
    return give, [jnp.clip(value.astype(I32), 0, limit) for value, limit in zip(rows, limits)]


def spread(value, target, direction, masks):
    height, columns = value.shape
    half = TAPS // 2
    for v in range(TAPS):
        shift = direction * (v - half)
        part = value
        if shift != 0:
            part = jnp.where(masks[shift + half], pltpu.roll(value, shift % columns, 1), 0.0)
        target[pl.ds(v * height, height), :] = part.astype(BF16)


def apply(operator, shifted):
    both = jnp.dot(operator, shifted, preferred_element_type=F32)
    height = both.shape[0] // 2
    return both[:height] + both[height:]


def build_operators(taps, expanded, operators, height):
    banks, lanes = taps.shape
    used = 2 * NPSF * TAPS
    group_row = floor_div(iota((lanes, lanes), 0), TAPS)
    group_column = floor_div(iota((lanes, lanes), 1), TAPS)
    lane = iota((lanes, lanes), 1)
    together = jnp.where((group_row == group_column) & (lane < used), 1.0, 0.0)
    raw = taps[...]
    sums = jnp.dot(raw, together, precision=lax.Precision.HIGHEST, preferred_element_type=F32)
    scaled = jnp.where(iota((banks, lanes), 1) < used, raw / jnp.where(sums > 0.0, sums, 1.0), 0.0)
    scaled = scaled.astype(BF16)
    depth = operators.shape[-1]
    tap_of = floor_div(iota((lanes, depth), 1), height).astype(I32)
    column_taps = []
    for j in range(NPSF):
        pick = (iota((lanes, depth), 0) == (NPSF + j) * TAPS + tap_of) & (tap_of < TAPS)
        pick = jnp.where(pick, 1.0, 0.0).astype(BF16)
        column_taps.append(jnp.dot(scaled, pick, preferred_element_type=F32))
    scaled = scaled.astype(F32)
    for u in range(TAPS):
        kernel = jnp.zeros((banks, depth), F32)
        for j in range(NPSF):
            at = j * TAPS + u
            kernel = kernel + scaled[:, at : at + 1] * column_taps[j]
        kernel = kernel * (1.0 / NPSF)
        coarse = kernel.astype(BF16).astype(F32)
        expanded[u, :, :] = coarse
        expanded[TAPS + u, :, :] = kernel - coarse
    lane = iota((height, depth), 1)
    tap = floor_div(lane, height).astype(I32)
    difference = iota((height, depth), 0) - (lane - tap * height)
    inside = tap < TAPS
    half = TAPS // 2

    def one_bank(b, carry):
        for part in range(2):
            ways = [jnp.zeros((height, depth), F32) for _ in range(2)]
            for u in range(TAPS):
                value = expanded[part * TAPS + u, pl.ds(b, 1), :]
                ways[0] = jnp.where(inside & (difference == u - half), value, ways[0])
                ways[1] = jnp.where(inside & (difference == half - u), value, ways[1])
            for way in range(2):
                operators[b, way, pl.ds(part * height, height), :] = ways[way].astype(BF16)
        return carry

    lax.fori_loop(0, banks, one_bank, 0)


def kernel(tile_rows, band_count, unroll, batch_in, weight_in, lo_in, hi_in, step_in, plane_in, row_in, cover_in,
           slot_in, start_in, stop_in, psf_in, exposures, model, updated, residual, batch, weight, lo, hi, step, plane,
           row, cover, slot, start, stop, psf, observed, image, grad, gathered, stamps, forward, backward, rows_out,
           leaving, landing, taps_out, taps_in, taps, expanded, operators, tables, targets, plane_ids, plane_of,
           indices, send_sems, recv_sems, own_sems):
    me = lax.axis_index("sky")
    peers, capacity = plane.shape
    total, columns = image.shape
    count, height, _ = observed.shape
    rows_each = landing.shape[2]
    meets = slot.shape[0]
    width = tables.shape[1]
    own_banks = psf.shape[0]
    half = TAPS // 2
    last = peers - 1

    barrier = pltpu.get_barrier_semaphore()

    def greet(i, carry):
        pl.semaphore_signal(
            barrier, inc=1, device_id={"sky": partner(me, i, peers)}, device_id_type=pl.DeviceIdType.MESH
        )
        return carry

    lax.fori_loop(1, peers, greet, 0)
    pairs = [(plane_in, plane), (row_in, row), (cover_in, cover), (slot_in, slot), (start_in, start), (stop_in, stop),
             (psf_in, psf), (model, image), (batch_in, batch), (weight_in, weight), (lo_in, lo), (hi_in, hi),
             (step_in, step), (exposures, observed)]
    copies = [pltpu.make_async_copy(a, b, own_sems.at[n]) for n, (a, b) in enumerate(pairs)]
    for copy in copies:
        copy.start()
    for copy in copies[:7]:
        copy.wait()

    chosen, used_rows = send_table(plane[...], row[...], cover[...], width, tile_rows)
    tables[pl.ds(0, peers), :] = jnp.clip(chosen, 0, total - 1)
    of_plane = floor_div(chosen, tile_rows)
    plane_ids[...] = of_plane
    targets[...] = jnp.where(used_rows, chosen - of_plane.astype(I32) * tile_rows, -1)
    give, at_rows = use_tables(slot[...], start[...], stop[...], peers, capacity, rows_each, width, height)
    tables[pl.ds(peers, peers), :] = give
    for k, value in enumerate(at_rows):
        tables[pl.ds(2 * peers + k, 1), pl.ds(0, count)] = value
    index_copy = pltpu.make_async_copy(tables, indices, own_sems.at[len(pairs)])
    index_copy.start()

    taps_out[...] = jnp.zeros(taps_out.shape, F32)
    taps_out[pl.ds(0, own_banks), pl.ds(0, psf.shape[1])] = psf[...]
    gathered[pl.ds(0, height), :] = jnp.zeros((height, columns), F32)
    gathered[pl.ds(height + peers * rows_each, height), :] = jnp.zeros((height, columns), F32)
    used = TAPS * height
    spare = forward.shape[1] - used
    if spare:
        for i in range(unroll):
            forward[i, pl.ds(used, spare), :] = jnp.zeros((spare, columns), BF16)
            backward[i, pl.ds(used, spare), :] = jnp.zeros((spare, columns), BF16)
    position = iota((height, columns), 0)
    lane = iota((height, columns), 1)
    masks = [
        (lane >= shift) if shift > 0 else (lane < columns + shift) for shift in range(-half, half + 1)
    ]
    index_copy.wait()
    copies[7].wait()

    def remote(phase, i):
        to = partner(me, i, peers)
        return pltpu.make_async_remote_copy(
            src_ref=leaving.at[phase, to],
            dst_ref=landing.at[phase, me],
            send_sem=send_sems.at[phase, i],
            recv_sem=recv_sems.at[phase, i],
            device_id={"sky": to},
            device_id_type=pl.DeviceIdType.MESH,
        )

    def remote_taps(i):
        return pltpu.make_async_remote_copy(
            src_ref=taps_out,
            dst_ref=taps_in.at[me],
            send_sem=send_sems.at[2 * ITERS, i],
            recv_sem=recv_sems.at[2 * ITERS, i],
            device_id={"sky": partner(me, i, peers)},
            device_id_type=pl.DeviceIdType.MESH,
        )

    def pick_rows(source, table_first, to):
        for p in range(rows_each):
            rows_out[pl.ds(p, 1), :] = source[pl.ds(indices[table_first + to, p], 1), :]
        return rows_out[...].astype(BF16)

    def send_all(phase, source, table_first):
        def one(t, carry):
            i = last - t
            to = partner(me, i, peers)
            leaving[phase, to, :, :] = pick_rows(source, table_first, to)

            @pl.when(t > 0)
            def _():
                remote(phase, i + 1).start()

            return carry

        lax.fori_loop(0, last, one, 0)
        landing[phase, me, :, :] = pick_rows(source, table_first, me)
        remote(phase, 1).start()

    def wait_barrier():
        pl.semaphore_wait(barrier, last)

        def one(t, carry):
            remote_taps(last - t).start()
            return carry

        lax.fori_loop(0, last, one, 0)
        taps_in[me, :, :] = taps_out[...]

    def take_taps():
        def one(t, carry):
            remote_taps(last - t).wait_recv()
            return carry

        lax.fori_loop(0, last, one, 0)

        def place(o, carry):
            taps[pl.ds(o * own_banks, own_banks), :] = taps_in[o, pl.ds(0, own_banks), :]
            return carry

        lax.fori_loop(0, peers, place, 0)
        build_operators(taps, expanded, operators, height)
        for copy in copies[8:]:
            copy.wait()

    def take_pieces(phase):
        def one(t, carry):
            i = last - t
            origin = partner(me, i, peers)

            @pl.when(i > 0)
            def _():
                remote(phase, i).wait_recv()

            here = pl.multiple_of(height + origin * rows_each, 8)
            gathered[pl.ds(here, rows_each), :] = landing[phase, origin].astype(F32)
            return carry

        lax.fori_loop(0, peers, one, 0)

    def assemble(e):
        value = None
        for k in range(meets):
            piece = gathered[pl.ds(indices[2 * peers + k, e], height), :]
            first = indices[2 * peers + meets + k, e]
            value = piece if value is None else jnp.where(position >= first, piece, value)
        return value

    def deblend():
        def group(g, carry):
            which = [g * unroll + i for i in range(unroll)]
            for i, e in enumerate(which):
                spread(assemble(e), forward.at[i], 1, masks)
            for i, e in enumerate(which):
                predicted = apply(operators[batch[e], 0], forward[i])
                error = weight[e] * (predicted - observed[e].astype(F32))
                residual[e] = error
                spread(error, backward.at[i], -1, masks)
            for i, e in enumerate(which):
                here = pl.multiple_of(e * height, 8)
                stamps[pl.ds(here, height), :] = apply(operators[batch[e], 1], backward[i])
            return carry

        lax.fori_loop(0, count // unroll, group, 0)

    together = 4 if rows_each % 128 == 0 and peers % 4 == 0 else 1
    planes = total // tile_rows
    wide = 2 if planes % 2 == 0 else 1

    def spread_planes():
        eye = iota((rows_each, width), 0) == iota((rows_each, width), 1)

        def one(o, carry):
            ids = jnp.where(eye, plane_ids[pl.ds(o, 1), :], 0.0)
            ids = jnp.sum(ids, axis=1, keepdims=True)
            plane_of[o, :, :] = jnp.broadcast_to(ids, (rows_each, columns)).astype(BF16)
            return carry

        lax.fori_loop(0, peers, one, 0)

    def clear():
        def one(p, carry):
            grad[p, :, :] = jnp.zeros((tile_rows, columns), F32)
            return carry

        lax.fori_loop(0, planes, one, 0)

    def joined(values, axis):
        return values[0] if len(values) == 1 else jnp.concatenate(values, axis=axis)

    def add_returned(phase):
        def one(q, carry):
            names, parts, owners = [], [], []
            for j in range(together):
                i = last - (q * together + j)
                origin = partner(me, i, peers)

                @pl.when(i > 0)
                def _():
                    remote(phase, i).wait_recv()

                names.append(targets[pl.ds(origin, 1), :][:, :rows_each])
                parts.append(landing[phase, origin])
                owners.append(plane_of[origin])
            name, part, owner = joined(names, 1), joined(parts, 0), joined(owners, 0)
            hit = iota((tile_rows, name.shape[1]), 0) == name
            chosen = jnp.where(hit, 1.0, 0.0).astype(BF16)
            for p in range(0, planes, wide):
                mine = [jnp.where(owner == float(p + w), part, jnp.zeros_like(part)) for w in range(wide)]
                both = jnp.dot(chosen, joined(mine, 1), preferred_element_type=F32)
                for w in range(wide):
                    grad[p + w, :, :] += both[:, w * columns : (w + 1) * columns]
            return carry

        lax.fori_loop(0, peers // together, one, 0)

    tile_position = iota((tile_rows, columns), 0)

    def move(target):
        def one_plane(p, carry):
            tile = lax.div(p, band_count)
            here = pl.ds(pl.multiple_of(p * tile_rows, 8), tile_rows)
            moved = jnp.maximum(image[here, :] - step[lax.rem(p, band_count)] * grad[p], 0.0)
            moved = jnp.where((tile_position >= lo[tile]) & (tile_position < hi[tile]), moved, 0.0)
            target[here, :] = moved
            return carry

        lax.fori_loop(0, total // tile_rows, one_plane, 0)

    wait_barrier()
    for sweep in range(ITERS):
        send_all(2 * sweep, image, 0)
        if sweep == 0:
            spread_planes()
            take_taps()
        take_pieces(2 * sweep)
        deblend()
        send_all(2 * sweep + 1, stamps, peers)
        clear()
        add_returned(2 * sweep + 1)
        move(updated if sweep == ITERS - 1 else image)

    def drain(t, carry):
        for phase in range(2 * ITERS):
            remote(phase, last - t).wait_send()
        remote_taps(last - t).wait_send()
        return carry

    lax.fori_loop(0, last, drain, 0)


def body(model, exposures, inv_var, step_size, psf_taps, exp_batch, send_plane, send_row, send_cover, use_slot,
         use_start, use_stop, foot_lo, foot_hi):
    tile_count, band_count, tile_rows, columns = model.shape
    count, height, _ = exposures.shape
    peers, capacity = send_plane.shape
    meets = use_slot.shape[1]
    rows_each = capacity * height // 2
    total = tile_count * band_count * tile_rows
    packed_rows = peers * rows_each
    own_banks = psf_taps.shape[0]
    tap_rows = round_up(own_banks, 8)
    depth = round_up(TAPS * height, 128)
    unroll = 32 if count % 32 == 0 else 1
    width = round_up(max(rows_each, count), 128)
    table_rows = 2 * peers + round_up(2 * meets, 8)
    banks = peers * own_banks
    operands = (exp_batch, inv_var, foot_lo, foot_hi, step_size, send_plane, send_row, send_cover, use_slot.T,
                use_start.T, use_stop.T, psf_taps, exposures, model.reshape(total, columns))
    updated, residual = pl.pallas_call(
        functools.partial(kernel, tile_rows, band_count, unroll),
        out_shape=(
            jax.ShapeDtypeStruct((total, columns), F32),
            jax.ShapeDtypeStruct(exposures.shape, F32),
        ),
        in_specs=[hbm()] * len(operands),
        out_specs=(vmem(), vmem()),
        scratch_shapes=[pltpu.SMEM(value.shape, value.dtype) for value in operands[:5]]
        + [pltpu.VMEM(value.shape, value.dtype) for value in operands[5:]]
        + [
            pltpu.VMEM((tile_count * band_count, tile_rows, columns), F32),
            pltpu.VMEM((packed_rows + 2 * height, columns), F32),
            pltpu.VMEM((count * height, columns), F32),
            pltpu.VMEM((unroll, depth, columns), BF16),
            pltpu.VMEM((unroll, depth, columns), BF16),
            pltpu.VMEM((rows_each, columns), F32),
            pltpu.VMEM((2 * ITERS, peers, rows_each, columns), BF16),
            pltpu.VMEM((2 * ITERS, peers, rows_each, columns), BF16),
            pltpu.VMEM((tap_rows, 128), F32),
            pltpu.VMEM((peers, tap_rows, 128), F32),
            pltpu.VMEM((banks, 128), F32),
            pltpu.VMEM((2 * TAPS, banks, depth), F32),
            pltpu.VMEM((banks, 2, 2 * height, depth), BF16),
            pltpu.VMEM((table_rows, width), I32),
            pltpu.VMEM((peers, width), I32),
            pltpu.VMEM((peers, width), F32),
            pltpu.VMEM((peers, rows_each, columns), BF16),
            pltpu.SMEM((table_rows, width), I32),
            pltpu.SemaphoreType.DMA((2 * ITERS + 1, peers)),
            pltpu.SemaphoreType.DMA((2 * ITERS + 1, peers)),
            pltpu.SemaphoreType.DMA((len(operands) + 1,)),
        ],
        compiler_params=pltpu.CompilerParams(
            collective_id=0, has_side_effects=True, vmem_limit_bytes=24 * 1024 * 1024
        ),
        name="deblend",
    )(*[pltpu.with_memory_space_constraint(value, pltpu.HBM) for value in operands])
    return updated.reshape(model.shape), residual


def solution(mesh):
    both = ("groups", "sky")
    return jax.shard_map(
        body,
        mesh=mesh,
        in_specs=(
            P(both, None, None, None),
            P(both, None, None),
            P(both),
            P(),
            P(both, None),
            P(both),
            P(both, None),
            P(both, None),
            P(both, None),
            P(both, None),
            P(both, None),
            P(both, None),
            P(both),
            P(both),
        ),
        out_specs=(P(both, None, None, None), P(both, None, None)),
        check_vma=False,
    )
```

```python
import functools

import jax
import jax.numpy as jnp
from jax import lax
from jax.experimental import pallas as pl
from jax.experimental.pallas import tpu as pltpu
from jax.sharding import PartitionSpec as P

NPSF = 4
TAPS = 7
ITERS = 2
F32 = jnp.float32
BF16 = jnp.bfloat16
I32 = jnp.int32


def vmem():
    return pl.BlockSpec(memory_space=pltpu.VMEM)


def hbm():
    return pl.BlockSpec(memory_space=pltpu.HBM)


def round_up(value, multiple):
    return -(-value // multiple) * multiple


def partner(me, i, peers):
    other = 0
    bit = 1
    while bit < peers:
        other = other + lax.rem(lax.div(me, bit) + lax.div(i, bit), 2) * bit
        bit *= 2
    return other


def iota(shape, axis):
    return lax.broadcasted_iota(I32, shape, axis)


def floor_div(value, divisor):
    return jnp.floor((value.astype(F32) + 0.5) * (1.0 / divisor))


def send_table(plane, row, cover, width, tile_rows):
    peers, capacity = plane.shape
    position = iota((peers, width), 1)
    chosen = jnp.zeros((peers, width), I32)
    offset = jnp.zeros((peers, 1), I32)
    for c in range(capacity):
        first = jnp.maximum(plane[:, c : c + 1], 0) * tile_rows + row[:, c : c + 1] - offset
        chosen = jnp.where(position >= offset, first + position, chosen)
        offset = offset + cover[:, c : c + 1]
    return chosen, position < offset


def use_tables(slot, start, stop, peers, capacity, rows_each, width, height):
    meets, count = slot.shape
    which_peer = iota((peers, count), 0).astype(F32)
    exposure = iota((1, count), 1).astype(F32)
    owners, columns, starts, lengths, alive, peer_rows = [], [], [], [], [], []
    for k in range(meets):
        name = slot[k : k + 1, :].astype(F32)
        peer = floor_div(name, capacity)
        owners.append(jnp.where(which_peer == peer, 1.0, 0.0))
        columns.append(name - peer * capacity)
        starts.append(start[k : k + 1, :].astype(F32))
        lengths.append(stop[k : k + 1, :].astype(F32) - starts[k])
        alive.append(name >= 0.0)
        peer_rows.append(peer)
    begin = jnp.zeros((peers, 1), F32)
    found = [jnp.zeros((1, count), F32) for _ in range(meets)]
    position = iota((peers, width), 1).astype(F32)
    chosen = jnp.zeros((peers, width), F32)
    for c in range(capacity):
        length = jnp.zeros((peers, count), F32)
        source = jnp.zeros((peers, count), F32)
        for k in range(meets):
            here = jnp.where(columns[k] == c, owners[k], 0.0)
            length = length + here * lengths[k]
            source = source + here * (exposure * height + starts[k])
            found[k] = found[k] + jnp.sum(here * begin, axis=0, keepdims=True)
        source = jnp.sum(source, axis=1, keepdims=True)
        chosen = jnp.where(position >= begin, source - begin + position, chosen)
        begin = begin + jnp.sum(length, axis=1, keepdims=True)
    give = jnp.clip(chosen.astype(I32), 0, count * height - 1)
    rows = []
    for k in range(meets):
        where = height + peer_rows[k] * rows_each + found[k] - starts[k]
        rows.append(jnp.where(alive[k], where, float(height)))
    for k in range(meets):
        rows.append(jnp.where(alive[k], starts[k], float(height)))
    limits = [peers * rows_each + height] * meets + [height] * meets
    return give, [jnp.clip(value.astype(I32), 0, limit) for value, limit in zip(rows, limits)]


def spread(value, target, direction, masks):
    height, columns = value.shape
    half = TAPS // 2
    for v in range(TAPS):
        shift = direction * (v - half)
        part = value
        if shift != 0:
            part = jnp.where(masks[shift + half], pltpu.roll(value, shift % columns, 1), 0.0)
        target[pl.ds(v * height, height), :] = part.astype(BF16)


def apply(operator, shifted):
    both = jnp.dot(operator, shifted, preferred_element_type=F32)
    height = both.shape[0] // 2
    return both[:height] + both[height:]


def build_operators(taps, expanded, operators, height):
    banks, lanes = taps.shape
    used = 2 * NPSF * TAPS
    group_row = floor_div(iota((lanes, lanes), 0), TAPS)
    group_column = floor_div(iota((lanes, lanes), 1), TAPS)
    lane = iota((lanes, lanes), 1)
    together = jnp.where((group_row == group_column) & (lane < used), 1.0, 0.0)
    raw = taps[...]
    sums = jnp.dot(raw, together, precision=lax.Precision.HIGHEST, preferred_element_type=F32)
    scaled = jnp.where(iota((banks, lanes), 1) < used, raw / jnp.where(sums > 0.0, sums, 1.0), 0.0)
    scaled = scaled.astype(BF16)
    depth = operators.shape[-1]
    tap_of = floor_div(iota((lanes, depth), 1), height).astype(I32)
    column_taps = []
    for j in range(NPSF):
        pick = (iota((lanes, depth), 0) == (NPSF + j) * TAPS + tap_of) & (tap_of < TAPS)
        pick = jnp.where(pick, 1.0, 0.0).astype(BF16)
        column_taps.append(jnp.dot(scaled, pick, preferred_element_type=F32))
    scaled = scaled.astype(F32)
    for u in range(TAPS):
        kernel = jnp.zeros((banks, depth), F32)
        for j in range(NPSF):
            at = j * TAPS + u
            kernel = kernel + scaled[:, at : at + 1] * column_taps[j]
        kernel = kernel * (1.0 / NPSF)
        coarse = kernel.astype(BF16).astype(F32)
        expanded[u, :, :] = coarse
        expanded[TAPS + u, :, :] = kernel - coarse
    lane = iota((height, depth), 1)
    tap = floor_div(lane, height).astype(I32)
    difference = iota((height, depth), 0) - (lane - tap * height)
    inside = tap < TAPS
    half = TAPS // 2

    def one_bank(b, carry):
        for part in range(2):
            ways = [jnp.zeros((height, depth), F32) for _ in range(2)]
            for u in range(TAPS):
                value = expanded[part * TAPS + u, pl.ds(b, 1), :]
                ways[0] = jnp.where(inside & (difference == u - half), value, ways[0])
                ways[1] = jnp.where(inside & (difference == half - u), value, ways[1])
            for way in range(2):
                operators[b, way, pl.ds(part * height, height), :] = ways[way].astype(BF16)
        return carry

    lax.fori_loop(0, banks, one_bank, 0)


def kernel(tile_rows, band_count, unroll, batch_in, weight_in, lo_in, hi_in, step_in, plane_in, row_in, cover_in,
           slot_in, start_in, stop_in, psf_in, exposures, model, updated, residual, batch, weight, lo, hi, step, plane,
           row, cover, slot, start, stop, psf, observed, image, grad, gathered, stamps, forward, backward, rows_out,
           leaving, landing, taps_out, taps_in, taps, expanded, operators, tables, targets, plane_ids, plane_of,
           indices, send_sems, recv_sems, own_sems):
    me = lax.axis_index("sky")
    peers, capacity = plane.shape
    total, columns = image.shape
    count, height, _ = observed.shape
    rows_each = landing.shape[2]
    meets = slot.shape[0]
    width = tables.shape[1]
    own_banks = psf.shape[0]
    half = TAPS // 2
    last = peers - 1

    barrier = pltpu.get_barrier_semaphore()

    def greet(i, carry):
        pl.semaphore_signal(
            barrier, inc=1, device_id={"sky": partner(me, i, peers)}, device_id_type=pl.DeviceIdType.MESH
        )
        return carry

    lax.fori_loop(1, peers, greet, 0)
    pairs = [(plane_in, plane), (row_in, row), (cover_in, cover), (slot_in, slot), (start_in, start), (stop_in, stop),
             (psf_in, psf), (model, image), (batch_in, batch), (weight_in, weight), (lo_in, lo), (hi_in, hi),
             (step_in, step), (exposures, observed)]
    copies = [pltpu.make_async_copy(a, b, own_sems.at[n]) for n, (a, b) in enumerate(pairs)]
    for copy in copies:
        copy.start()
    for copy in copies[:7]:
        copy.wait()

    chosen, used_rows = send_table(plane[...], row[...], cover[...], width, tile_rows)
    tables[pl.ds(0, peers), :] = jnp.clip(chosen, 0, total - 1)
    of_plane = floor_div(chosen, tile_rows)
    plane_ids[...] = of_plane
    targets[...] = jnp.where(used_rows, chosen - of_plane.astype(I32) * tile_rows, -1)
    give, at_rows = use_tables(slot[...], start[...], stop[...], peers, capacity, rows_each, width, height)
    tables[pl.ds(peers, peers), :] = give
    for k, value in enumerate(at_rows):
        tables[pl.ds(2 * peers + k, 1), pl.ds(0, count)] = value
    index_copy = pltpu.make_async_copy(tables, indices, own_sems.at[len(pairs)])
    index_copy.start()

    taps_out[...] = jnp.zeros(taps_out.shape, F32)
    taps_out[pl.ds(0, own_banks), pl.ds(0, psf.shape[1])] = psf[...]
    gathered[pl.ds(0, height), :] = jnp.zeros((height, columns), F32)
    gathered[pl.ds(height + peers * rows_each, height), :] = jnp.zeros((height, columns), F32)
    used = TAPS * height
    spare = forward.shape[1] - used
    if spare:
        for i in range(unroll):
            forward[i, pl.ds(used, spare), :] = jnp.zeros((spare, columns), BF16)
            backward[i, pl.ds(used, spare), :] = jnp.zeros((spare, columns), BF16)
    position = iota((height, columns), 0)
    lane = iota((height, columns), 1)
    masks = [
        (lane >= shift) if shift > 0 else (lane < columns + shift) for shift in range(-half, half + 1)
    ]
    index_copy.wait()
    copies[7].wait()

    def remote(phase, i):
        to = partner(me, i, peers)
        return pltpu.make_async_remote_copy(
            src_ref=leaving.at[phase, to],
            dst_ref=landing.at[phase, me],
            send_sem=send_sems.at[phase, i],
            recv_sem=recv_sems.at[phase, i],
            device_id={"sky": to},
            device_id_type=pl.DeviceIdType.MESH,
        )

    def remote_taps(i):
        return pltpu.make_async_remote_copy(
            src_ref=taps_out,
            dst_ref=taps_in.at[me],
            send_sem=send_sems.at[2 * ITERS, i],
            recv_sem=recv_sems.at[2 * ITERS, i],
            device_id={"sky": partner(me, i, peers)},
            device_id_type=pl.DeviceIdType.MESH,
        )

    def pick_rows(source, table_first, to):
        for p in range(rows_each):
            rows_out[pl.ds(p, 1), :] = source[pl.ds(indices[table_first + to, p], 1), :]
        return rows_out[...].astype(BF16)

    def send_all(phase, source, table_first):
        def one(t, carry):
            i = last - t
            to = partner(me, i, peers)
            leaving[phase, to, :, :] = pick_rows(source, table_first, to)

            @pl.when(t > 0)
            def _():
                remote(phase, i + 1).start()

            return carry

        lax.fori_loop(0, last, one, 0)
        landing[phase, me, :, :] = pick_rows(source, table_first, me)
        remote(phase, 1).start()

    def wait_barrier():
        pl.semaphore_wait(barrier, last)

        def one(t, carry):
            remote_taps(last - t).start()
            return carry

        lax.fori_loop(0, last, one, 0)
        taps_in[me, :, :] = taps_out[...]

    def take_taps():
        def one(t, carry):
            remote_taps(last - t).wait_recv()
            return carry

        lax.fori_loop(0, last, one, 0)

        def place(o, carry):
            taps[pl.ds(o * own_banks, own_banks), :] = taps_in[o, pl.ds(0, own_banks), :]
            return carry

        lax.fori_loop(0, peers, place, 0)
        build_operators(taps, expanded, operators, height)
        for copy in copies[8:]:
            copy.wait()

    quarter = peers // 4 if peers % 4 == 0 else peers

    def arrival(t):
        block = lax.div(t, quarter)
        return (lax.rem(3 * block, 5) - 2 * lax.div(block, 3)) * quarter + lax.rem(t, quarter)

    def take_pieces(phase):
        def one(t, carry):
            i = arrival(t)
            origin = partner(me, i, peers)

            @pl.when(i > 0)
            def _():
                remote(phase, i).wait_recv()

            here = pl.multiple_of(height + origin * rows_each, 8)
            gathered[pl.ds(here, rows_each), :] = landing[phase, origin].astype(F32)
            return carry

        lax.fori_loop(0, peers, one, 0)

    def assemble(e):
        value = None
        for k in range(meets):
            piece = gathered[pl.ds(indices[2 * peers + k, e], height), :]
            first = indices[2 * peers + meets + k, e]
            value = piece if value is None else jnp.where(position >= first, piece, value)
        return value

    def deblend():
        def group(g, carry):
            which = [g * unroll + i for i in range(unroll)]
            for i, e in enumerate(which):
                spread(assemble(e), forward.at[i], 1, masks)
            for i, e in enumerate(which):
                predicted = apply(operators[batch[e], 0], forward[i])
                error = weight[e] * (predicted - observed[e].astype(F32))
                residual[e] = error
                spread(error, backward.at[i], -1, masks)
            for i, e in enumerate(which):
                here = pl.multiple_of(e * height, 8)
                stamps[pl.ds(here, height), :] = apply(operators[batch[e], 1], backward[i])
            return carry

        lax.fori_loop(0, count // unroll, group, 0)

    together = 4 if rows_each % 128 == 0 and peers % 4 == 0 else 1
    planes = total // tile_rows
    wide = 2 if planes % 2 == 0 else 1

    def spread_planes():
        eye = iota((rows_each, width), 0) == iota((rows_each, width), 1)

        def one(o, carry):
            ids = jnp.where(eye, plane_ids[pl.ds(o, 1), :], 0.0)
            ids = jnp.sum(ids, axis=1, keepdims=True)
            plane_of[o, :, :] = jnp.broadcast_to(ids, (rows_each, columns)).astype(BF16)
            return carry

        lax.fori_loop(0, peers, one, 0)

    def clear():
        def one(p, carry):
            grad[p, :, :] = jnp.zeros((tile_rows, columns), F32)
            return carry

        lax.fori_loop(0, planes, one, 0)

    def joined(values, axis):
        return values[0] if len(values) == 1 else jnp.concatenate(values, axis=axis)

    def add_returned(phase):
        def one(q, carry):
            names, parts, owners = [], [], []
            for j in range(together):
                i = arrival(q * together + j)
                origin = partner(me, i, peers)

                @pl.when(i > 0)
                def _():
                    remote(phase, i).wait_recv()

                names.append(targets[pl.ds(origin, 1), :][:, :rows_each])
                parts.append(landing[phase, origin])
                owners.append(plane_of[origin])
            name, part, owner = joined(names, 1), joined(parts, 0), joined(owners, 0)
            hit = iota((tile_rows, name.shape[1]), 0) == name
            chosen = jnp.where(hit, 1.0, 0.0).astype(BF16)
            for p in range(0, planes, wide):
                mine = [jnp.where(owner == float(p + w), part, jnp.zeros_like(part)) for w in range(wide)]
                both = jnp.dot(chosen, joined(mine, 1), preferred_element_type=F32)
                for w in range(wide):
                    grad[p + w, :, :] += both[:, w * columns : (w + 1) * columns]
            return carry

        lax.fori_loop(0, peers // together, one, 0)

    tile_position = iota((tile_rows, columns), 0)

    def move(target):
        def one_plane(p, carry):
            tile = lax.div(p, band_count)
            here = pl.ds(pl.multiple_of(p * tile_rows, 8), tile_rows)
            moved = jnp.maximum(image[here, :] - step[lax.rem(p, band_count)] * grad[p], 0.0)
            moved = jnp.where((tile_position >= lo[tile]) & (tile_position < hi[tile]), moved, 0.0)
            target[here, :] = moved
            return carry

        lax.fori_loop(0, total // tile_rows, one_plane, 0)

    wait_barrier()
    for sweep in range(ITERS):
        send_all(2 * sweep, image, 0)
        if sweep == 0:
            spread_planes()
            take_taps()
        take_pieces(2 * sweep)
        deblend()
        send_all(2 * sweep + 1, stamps, peers)
        clear()
        add_returned(2 * sweep + 1)
        move(updated if sweep == ITERS - 1 else image)

    def drain(t, carry):
        for phase in range(2 * ITERS):
            remote(phase, last - t).wait_send()
        remote_taps(last - t).wait_send()
        return carry

    lax.fori_loop(0, last, drain, 0)


def emit_kernel(updated, residual, updated_out, residual_out, sems):
    copies = []
    for source, target in ((updated, updated_out), (residual, residual_out)):
        rows = source.shape[0] // 4
        for n in range(4):
            part = pl.ds(n * rows, rows)
            copies.append(pltpu.make_async_copy(source.at[part], target.at[part], sems.at[len(copies)]))
            copies[-1].start()
    for copy in copies:
        copy.wait()


def body(model, exposures, inv_var, step_size, psf_taps, exp_batch, send_plane, send_row, send_cover, use_slot,
         use_start, use_stop, foot_lo, foot_hi):
    tile_count, band_count, tile_rows, columns = model.shape
    count, height, _ = exposures.shape
    peers, capacity = send_plane.shape
    meets = use_slot.shape[1]
    rows_each = capacity * height // 2
    total = tile_count * band_count * tile_rows
    packed_rows = peers * rows_each
    own_banks = psf_taps.shape[0]
    tap_rows = round_up(own_banks, 8)
    depth = round_up(TAPS * height, 128)
    unroll = 32 if count % 32 == 0 else 1
    width = round_up(max(rows_each, count), 128)
    table_rows = 2 * peers + round_up(2 * meets, 8)
    banks = peers * own_banks
    operands = (exp_batch, inv_var, foot_lo, foot_hi, step_size, send_plane, send_row, send_cover, use_slot.T,
                use_start.T, use_stop.T, psf_taps, exposures, model.reshape(total, columns))
    updated, residual = pl.pallas_call(
        functools.partial(kernel, tile_rows, band_count, unroll),
        out_shape=(
            jax.ShapeDtypeStruct((total, columns), F32),
            jax.ShapeDtypeStruct(exposures.shape, F32),
        ),
        in_specs=[hbm()] * len(operands),
        out_specs=(vmem(), vmem()),
        scratch_shapes=[pltpu.SMEM(value.shape, value.dtype) for value in operands[:5]]
        + [pltpu.VMEM(value.shape, value.dtype) for value in operands[5:]]
        + [
            pltpu.VMEM((tile_count * band_count, tile_rows, columns), F32),
            pltpu.VMEM((packed_rows + 2 * height, columns), F32),
            pltpu.VMEM((count * height, columns), F32),
            pltpu.VMEM((unroll, depth, columns), BF16),
            pltpu.VMEM((unroll, depth, columns), BF16),
            pltpu.VMEM((rows_each, columns), F32),
            pltpu.VMEM((2 * ITERS, peers, rows_each, columns), BF16),
            pltpu.VMEM((2 * ITERS, peers, rows_each, columns), BF16),
            pltpu.VMEM((tap_rows, 128), F32),
            pltpu.VMEM((peers, tap_rows, 128), F32),
            pltpu.VMEM((banks, 128), F32),
            pltpu.VMEM((2 * TAPS, banks, depth), F32),
            pltpu.VMEM((banks, 2, 2 * height, depth), BF16),
            pltpu.VMEM((table_rows, width), I32),
            pltpu.VMEM((peers, width), I32),
            pltpu.VMEM((peers, width), F32),
            pltpu.VMEM((peers, rows_each, columns), BF16),
            pltpu.SMEM((table_rows, width), I32),
            pltpu.SemaphoreType.DMA((2 * ITERS + 1, peers)),
            pltpu.SemaphoreType.DMA((2 * ITERS + 1, peers)),
            pltpu.SemaphoreType.DMA((len(operands) + 1,)),
        ],
        compiler_params=pltpu.CompilerParams(
            collective_id=0, has_side_effects=True, vmem_limit_bytes=24 * 1024 * 1024
        ),
        name="deblend",
    )(*[pltpu.with_memory_space_constraint(value, pltpu.HBM) for value in operands])
    updated, residual = pl.pallas_call(
        emit_kernel,
        out_shape=(
            jax.ShapeDtypeStruct((total, columns), F32),
            jax.ShapeDtypeStruct(exposures.shape, F32),
        ),
        in_specs=[vmem()] * 2,
        out_specs=(hbm(), hbm()),
        scratch_shapes=[pltpu.SemaphoreType.DMA((8,))],
        compiler_params=pltpu.CompilerParams(vmem_limit_bytes=1024 * 1024),
        name="emit",
    )(updated, residual)
    return updated.reshape(model.shape), residual


def solution(mesh):
    both = ("groups", "sky")
    return jax.shard_map(
        body,
        mesh=mesh,
        in_specs=(
            P(both, None, None, None),
            P(both, None, None),
            P(both),
            P(),
            P(both, None),
            P(both),
            P(both, None),
            P(both, None),
            P(both, None),
            P(both, None),
            P(both, None),
            P(both, None),
            P(both),
            P(both),
        ),
        out_specs=(P(both, None, None, None), P(both, None, None)),
        check_vma=False,
    )
```

```python
import functools

import jax
import jax.numpy as jnp
from jax import lax
from jax.experimental import pallas as pl
from jax.experimental.pallas import tpu as pltpu
from jax.sharding import PartitionSpec as P

NPSF = 4
TAPS = 7
ITERS = 2
F32 = jnp.float32
BF16 = jnp.bfloat16
I32 = jnp.int32


def vmem():
    return pl.BlockSpec(memory_space=pltpu.VMEM)


def hbm():
    return pl.BlockSpec(memory_space=pltpu.HBM)


def round_up(value, multiple):
    return -(-value // multiple) * multiple


def partner(me, i, peers):
    other = 0
    bit = 1
    while bit < peers:
        other = other + lax.rem(lax.div(me, bit) + lax.div(i, bit), 2) * bit
        bit *= 2
    return other


def iota(shape, axis):
    return lax.broadcasted_iota(I32, shape, axis)


def floor_div(value, divisor):
    return jnp.floor((value.astype(F32) + 0.5) * (1.0 / divisor))


def send_table(plane, row, cover, width, tile_rows):
    peers, capacity = plane.shape
    position = iota((peers, width), 1)
    chosen = jnp.zeros((peers, width), I32)
    offset = jnp.zeros((peers, 1), I32)
    for c in range(capacity):
        first = jnp.maximum(plane[:, c : c + 1], 0) * tile_rows + row[:, c : c + 1] - offset
        chosen = jnp.where(position >= offset, first + position, chosen)
        offset = offset + cover[:, c : c + 1]
    return chosen, position < offset


def use_tables(slot, start, stop, peers, capacity, rows_each, width, height):
    meets, count = slot.shape
    which_peer = iota((peers, count), 0).astype(F32)
    exposure = iota((1, count), 1).astype(F32)
    owners, columns, starts, lengths, alive, peer_rows = [], [], [], [], [], []
    for k in range(meets):
        name = slot[k : k + 1, :].astype(F32)
        peer = floor_div(name, capacity)
        owners.append(jnp.where(which_peer == peer, 1.0, 0.0))
        columns.append(name - peer * capacity)
        starts.append(start[k : k + 1, :].astype(F32))
        lengths.append(stop[k : k + 1, :].astype(F32) - starts[k])
        alive.append(name >= 0.0)
        peer_rows.append(peer)
    begin = jnp.zeros((peers, 1), F32)
    found = [jnp.zeros((1, count), F32) for _ in range(meets)]
    position = iota((peers, width), 1).astype(F32)
    chosen = jnp.zeros((peers, width), F32)
    for c in range(capacity):
        length = jnp.zeros((peers, count), F32)
        source = jnp.zeros((peers, count), F32)
        for k in range(meets):
            here = jnp.where(columns[k] == c, owners[k], 0.0)
            length = length + here * lengths[k]
            source = source + here * (exposure * height + starts[k])
            found[k] = found[k] + jnp.sum(here * begin, axis=0, keepdims=True)
        source = jnp.sum(source, axis=1, keepdims=True)
        chosen = jnp.where(position >= begin, source - begin + position, chosen)
        begin = begin + jnp.sum(length, axis=1, keepdims=True)
    give = jnp.clip(chosen.astype(I32), 0, count * height - 1)
    rows = []
    for k in range(meets):
        where = height + peer_rows[k] * rows_each + found[k] - starts[k]
        rows.append(jnp.where(alive[k], where, float(height)))
    for k in range(meets):
        rows.append(jnp.where(alive[k], starts[k], float(height)))
    limits = [peers * rows_each + height] * meets + [height] * meets
    return give, [jnp.clip(value.astype(I32), 0, limit) for value, limit in zip(rows, limits)]


def spread(value, target, direction, masks):
    height, columns = value.shape
    half = TAPS // 2
    for v in range(TAPS):
        shift = direction * (v - half)
        part = value
        if shift != 0:
            part = jnp.where(masks[shift + half], pltpu.roll(value, shift % columns, 1), 0.0)
        target[pl.ds(v * height, height), :] = part.astype(BF16)


def apply(operator, shifted):
    both = jnp.dot(operator, shifted, preferred_element_type=F32)
    height = both.shape[0] // 2
    return both[:height] + both[height:]


def build_operators(taps, expanded, operators, height):
    banks, lanes = taps.shape
    used = 2 * NPSF * TAPS
    group_row = floor_div(iota((lanes, lanes), 0), TAPS)
    group_column = floor_div(iota((lanes, lanes), 1), TAPS)
    lane = iota((lanes, lanes), 1)
    together = jnp.where((group_row == group_column) & (lane < used), 1.0, 0.0)
    raw = taps[...]
    sums = jnp.dot(raw, together, precision=lax.Precision.HIGHEST, preferred_element_type=F32)
    scaled = jnp.where(iota((banks, lanes), 1) < used, raw / jnp.where(sums > 0.0, sums, 1.0), 0.0)
    scaled = scaled.astype(BF16)
    depth = operators.shape[-1]
    tap_of = floor_div(iota((lanes, depth), 1), height).astype(I32)
    column_taps = []
    for j in range(NPSF):
        pick = (iota((lanes, depth), 0) == (NPSF + j) * TAPS + tap_of) & (tap_of < TAPS)
        pick = jnp.where(pick, 1.0, 0.0).astype(BF16)
        column_taps.append(jnp.dot(scaled, pick, preferred_element_type=F32))
    scaled = scaled.astype(F32)
    for u in range(TAPS):
        kernel = jnp.zeros((banks, depth), F32)
        for j in range(NPSF):
            at = j * TAPS + u
            kernel = kernel + scaled[:, at : at + 1] * column_taps[j]
        kernel = kernel * (1.0 / NPSF)
        coarse = kernel.astype(BF16).astype(F32)
        expanded[u, :, :] = coarse
        expanded[TAPS + u, :, :] = kernel - coarse
    lane = iota((height, depth), 1)
    tap = floor_div(lane, height).astype(I32)
    difference = iota((height, depth), 0) - (lane - tap * height)
    inside = tap < TAPS
    half = TAPS // 2

    def one_bank(b, carry):
        for part in range(2):
            ways = [jnp.zeros((height, depth), F32) for _ in range(2)]
            for u in range(TAPS):
                value = expanded[part * TAPS + u, pl.ds(b, 1), :]
                ways[0] = jnp.where(inside & (difference == u - half), value, ways[0])
                ways[1] = jnp.where(inside & (difference == half - u), value, ways[1])
            for way in range(2):
                operators[b, way, pl.ds(part * height, height), :] = ways[way].astype(BF16)
        return carry

    lax.fori_loop(0, banks, one_bank, 0)


def kernel(tile_rows, band_count, unroll, batch_in, weight_in, lo_in, hi_in, step_in, plane_in, row_in, cover_in,
           slot_in, start_in, stop_in, psf_in, exposures, model, updated, residual, batch, weight, lo, hi, step, plane,
           row, cover, slot, start, stop, psf, observed, image, grad, gathered, stamps, forward, backward, rows_out,
           leaving, landing, taps_out, taps_in, taps, expanded, operators, tables, targets, plane_ids, plane_of,
           indices, send_sems, recv_sems, own_sems):
    me = lax.axis_index("sky")
    peers, capacity = plane.shape
    total, columns = image.shape
    count, height, _ = observed.shape
    rows_each = landing.shape[2]
    meets = slot.shape[0]
    width = tables.shape[1]
    own_banks = psf.shape[0]
    half = TAPS // 2
    last = peers - 1

    barrier = pltpu.get_barrier_semaphore()

    def greet(i, carry):
        pl.semaphore_signal(
            barrier, inc=1, device_id={"sky": partner(me, i, peers)}, device_id_type=pl.DeviceIdType.MESH
        )
        return carry

    lax.fori_loop(1, peers, greet, 0)
    pairs = [(plane_in, plane), (row_in, row), (cover_in, cover), (slot_in, slot), (start_in, start), (stop_in, stop),
             (psf_in, psf), (model, image), (batch_in, batch), (weight_in, weight), (lo_in, lo), (hi_in, hi),
             (step_in, step), (exposures, observed)]
    copies = [pltpu.make_async_copy(a, b, own_sems.at[n]) for n, (a, b) in enumerate(pairs)]
    for copy in copies:
        copy.start()
    for copy in copies[:7]:
        copy.wait()

    chosen, used_rows = send_table(plane[...], row[...], cover[...], width, tile_rows)
    tables[pl.ds(0, peers), :] = jnp.clip(chosen, 0, total - 1)
    of_plane = floor_div(chosen, tile_rows)
    plane_ids[...] = of_plane
    targets[...] = jnp.where(used_rows, chosen - of_plane.astype(I32) * tile_rows, -1)
    give, at_rows = use_tables(slot[...], start[...], stop[...], peers, capacity, rows_each, width, height)
    tables[pl.ds(peers, peers), :] = give
    for k, value in enumerate(at_rows):
        tables[pl.ds(2 * peers + k, 1), pl.ds(0, count)] = value
    index_copy = pltpu.make_async_copy(tables, indices, own_sems.at[len(pairs)])
    index_copy.start()

    taps_out[...] = jnp.zeros(taps_out.shape, F32)
    taps_out[pl.ds(0, own_banks), pl.ds(0, psf.shape[1])] = psf[...]
    gathered[pl.ds(0, height), :] = jnp.zeros((height, columns), F32)
    gathered[pl.ds(height + peers * rows_each, height), :] = jnp.zeros((height, columns), F32)
    used = TAPS * height
    spare = forward.shape[1] - used
    if spare:
        for i in range(unroll):
            forward[i, pl.ds(used, spare), :] = jnp.zeros((spare, columns), BF16)
            backward[i, pl.ds(used, spare), :] = jnp.zeros((spare, columns), BF16)
    position = iota((height, columns), 0)
    lane = iota((height, columns), 1)
    masks = [
        (lane >= shift) if shift > 0 else (lane < columns + shift) for shift in range(-half, half + 1)
    ]
    index_copy.wait()
    copies[7].wait()

    def remote(phase, i):
        to = partner(me, i, peers)
        return pltpu.make_async_remote_copy(
            src_ref=leaving.at[phase, to],
            dst_ref=landing.at[phase, me],
            send_sem=send_sems.at[phase, i],
            recv_sem=recv_sems.at[phase, i],
            device_id={"sky": to},
            device_id_type=pl.DeviceIdType.MESH,
        )

    def remote_taps(i):
        return pltpu.make_async_remote_copy(
            src_ref=taps_out,
            dst_ref=taps_in.at[me],
            send_sem=send_sems.at[2 * ITERS, i],
            recv_sem=recv_sems.at[2 * ITERS, i],
            device_id={"sky": partner(me, i, peers)},
            device_id_type=pl.DeviceIdType.MESH,
        )

    def pick_rows(source, table_first, to):
        for p in range(rows_each):
            rows_out[pl.ds(p, 1), :] = source[pl.ds(indices[table_first + to, p], 1), :]
        return rows_out[...].astype(BF16)

    def send_all(phase, source, table_first):
        def one(t, carry):
            i = last - t
            to = partner(me, i, peers)
            leaving[phase, to, :, :] = pick_rows(source, table_first, to)

            @pl.when(t > 0)
            def _():
                remote(phase, i + 1).start()

            return carry

        lax.fori_loop(0, last, one, 0)
        landing[phase, me, :, :] = pick_rows(source, table_first, me)
        remote(phase, 1).start()

    def wait_barrier():
        pl.semaphore_wait(barrier, last)

        def one(t, carry):
            remote_taps(last - t).start()
            return carry

        lax.fori_loop(0, last, one, 0)
        taps_in[me, :, :] = taps_out[...]

    def take_taps():
        def one(t, carry):
            remote_taps(last - t).wait_recv()
            return carry

        lax.fori_loop(0, last, one, 0)

        def place(o, carry):
            taps[pl.ds(o * own_banks, own_banks), :] = taps_in[o, pl.ds(0, own_banks), :]
            return carry

        lax.fori_loop(0, peers, place, 0)
        build_operators(taps, expanded, operators, height)
        for copy in copies[8:]:
            copy.wait()

    quarter = peers // 4 if peers % 4 == 0 else peers

    def arrival(t):
        block = lax.div(t, quarter)
        return (lax.rem(3 * block, 5) - 2 * lax.div(block, 3)) * quarter + lax.rem(t, quarter)

    def take_pieces(phase):
        def one(t, carry):
            i = arrival(t)
            origin = partner(me, i, peers)

            @pl.when(i > 0)
            def _():
                remote(phase, i).wait_recv()

            here = pl.multiple_of(height + origin * rows_each, 8)
            gathered[pl.ds(here, rows_each), :] = landing[phase, origin].astype(F32)
            return carry

        lax.fori_loop(0, peers, one, 0)

    def assemble(e):
        value = None
        for k in range(meets):
            piece = gathered[pl.ds(indices[2 * peers + k, e], height), :]
            first = indices[2 * peers + meets + k, e]
            value = piece if value is None else jnp.where(position >= first, piece, value)
        return value

    def deblend():
        def group(g, carry):
            which = [g * unroll + i for i in range(unroll)]
            for i, e in enumerate(which):
                spread(assemble(e), forward.at[i], 1, masks)
            for i, e in enumerate(which):
                predicted = apply(operators[batch[e], 0], forward[i])
                error = weight[e] * (predicted - observed[e].astype(F32))
                residual[e] = error
                spread(error, backward.at[i], -1, masks)
            for i, e in enumerate(which):
                here = pl.multiple_of(e * height, 8)
                stamps[pl.ds(here, height), :] = apply(operators[batch[e], 1], backward[i])
            return carry

        lax.fori_loop(0, count // unroll, group, 0)

    together = 4 if rows_each % 128 == 0 and peers % 4 == 0 else 1
    planes = total // tile_rows
    wide = 2 if planes % 2 == 0 else 1

    def spread_planes():
        eye = iota((rows_each, width), 0) == iota((rows_each, width), 1)

        def one(o, carry):
            ids = jnp.where(eye, plane_ids[pl.ds(o, 1), :], 0.0)
            ids = jnp.sum(ids, axis=1, keepdims=True)
            plane_of[o, :, :] = jnp.broadcast_to(ids, (rows_each, columns)).astype(BF16)
            return carry

        lax.fori_loop(0, peers, one, 0)

    def clear():
        def one(p, carry):
            grad[p, :, :] = jnp.zeros((tile_rows, columns), F32)
            return carry

        lax.fori_loop(0, planes, one, 0)

    def joined(values, axis):
        return values[0] if len(values) == 1 else jnp.concatenate(values, axis=axis)

    def add_returned(phase):
        def one(q, carry):
            names, parts, owners = [], [], []
            for j in range(together):
                i = arrival(q * together + j)
                origin = partner(me, i, peers)

                @pl.when(i > 0)
                def _():
                    remote(phase, i).wait_recv()

                names.append(targets[pl.ds(origin, 1), :][:, :rows_each])
                parts.append(landing[phase, origin])
                owners.append(plane_of[origin])
            name, part, owner = joined(names, 1), joined(parts, 0), joined(owners, 0)
            hit = iota((tile_rows, name.shape[1]), 0) == name
            chosen = jnp.where(hit, 1.0, 0.0).astype(BF16)
            for p in range(0, planes, wide):
                mine = [jnp.where(owner == float(p + w), part, jnp.zeros_like(part)) for w in range(wide)]
                both = jnp.dot(chosen, joined(mine, 1), preferred_element_type=F32)
                for w in range(wide):
                    grad[p + w, :, :] += both[:, w * columns : (w + 1) * columns]
            return carry

        lax.fori_loop(0, peers // together, one, 0)

    tile_position = iota((tile_rows, columns), 0)

    def move(target):
        def one_plane(p, carry):
            tile = lax.div(p, band_count)
            here = pl.ds(pl.multiple_of(p * tile_rows, 8), tile_rows)
            moved = jnp.maximum(image[here, :] - step[lax.rem(p, band_count)] * grad[p], 0.0)
            moved = jnp.where((tile_position >= lo[tile]) & (tile_position < hi[tile]), moved, 0.0)
            target[here, :] = moved
            return carry

        lax.fori_loop(0, total // tile_rows, one_plane, 0)

    wait_barrier()
    for sweep in range(ITERS):
        send_all(2 * sweep, image, 0)
        if sweep == 0:
            spread_planes()
            take_taps()
        take_pieces(2 * sweep)
        deblend()
        send_all(2 * sweep + 1, stamps, peers)
        clear()
        add_returned(2 * sweep + 1)
        move(updated if sweep == ITERS - 1 else image)

    def drain(t, carry):
        for phase in range(2 * ITERS):
            remote(phase, last - t).wait_send()
        remote_taps(last - t).wait_send()
        return carry

    lax.fori_loop(0, last, drain, 0)


def emit_kernel(updated, residual, updated_out, residual_out, sems):
    copies = []
    for source, target in ((updated, updated_out), (residual, residual_out)):
        rows = source.shape[0] // 4
        for n in range(4):
            part = pl.ds(n * rows, rows)
            copies.append(pltpu.make_async_copy(source.at[part], target.at[part], sems.at[len(copies)]))
            copies[-1].start()
    for copy in copies:
        copy.wait()


def body(model, exposures, inv_var, step_size, psf_taps, exp_batch, send_plane, send_row, send_cover, use_slot,
         use_start, use_stop, foot_lo, foot_hi):
    tile_count, band_count, tile_rows, columns = model.shape
    count, height, _ = exposures.shape
    peers, capacity = send_plane.shape
    meets = use_slot.shape[1]
    rows_each = capacity * height // 2
    total = tile_count * band_count * tile_rows
    packed_rows = peers * rows_each
    own_banks = psf_taps.shape[0]
    tap_rows = round_up(own_banks, 8)
    depth = round_up(TAPS * height, 128)
    unroll = 64 if count % 64 == 0 else 1
    width = round_up(max(rows_each, count), 128)
    table_rows = 2 * peers + round_up(2 * meets, 8)
    banks = peers * own_banks
    operands = (exp_batch, inv_var, foot_lo, foot_hi, step_size, send_plane, send_row, send_cover, use_slot.T,
                use_start.T, use_stop.T, psf_taps, exposures, model.reshape(total, columns))
    updated, residual = pl.pallas_call(
        functools.partial(kernel, tile_rows, band_count, unroll),
        out_shape=(
            jax.ShapeDtypeStruct((total, columns), F32),
            jax.ShapeDtypeStruct(exposures.shape, F32),
        ),
        in_specs=[hbm()] * len(operands),
        out_specs=(vmem(), vmem()),
        scratch_shapes=[pltpu.SMEM(value.shape, value.dtype) for value in operands[:5]]
        + [pltpu.VMEM(value.shape, value.dtype) for value in operands[5:]]
        + [
            pltpu.VMEM((tile_count * band_count, tile_rows, columns), F32),
            pltpu.VMEM((packed_rows + 2 * height, columns), F32),
            pltpu.VMEM((count * height, columns), F32),
            pltpu.VMEM((unroll, depth, columns), BF16),
            pltpu.VMEM((unroll, depth, columns), BF16),
            pltpu.VMEM((rows_each, columns), F32),
            pltpu.VMEM((2 * ITERS, peers, rows_each, columns), BF16),
            pltpu.VMEM((2 * ITERS, peers, rows_each, columns), BF16),
            pltpu.VMEM((tap_rows, 128), F32),
            pltpu.VMEM((peers, tap_rows, 128), F32),
            pltpu.VMEM((banks, 128), F32),
            pltpu.VMEM((2 * TAPS, banks, depth), F32),
            pltpu.VMEM((banks, 2, 2 * height, depth), BF16),
            pltpu.VMEM((table_rows, width), I32),
            pltpu.VMEM((peers, width), I32),
            pltpu.VMEM((peers, width), F32),
            pltpu.VMEM((peers, rows_each, columns), BF16),
            pltpu.SMEM((table_rows, width), I32),
            pltpu.SemaphoreType.DMA((2 * ITERS + 1, peers)),
            pltpu.SemaphoreType.DMA((2 * ITERS + 1, peers)),
            pltpu.SemaphoreType.DMA((len(operands) + 1,)),
        ],
        compiler_params=pltpu.CompilerParams(
            collective_id=0, has_side_effects=True, vmem_limit_bytes=24 * 1024 * 1024
        ),
        name="deblend",
    )(*[pltpu.with_memory_space_constraint(value, pltpu.HBM) for value in operands])
    updated, residual = pl.pallas_call(
        emit_kernel,
        out_shape=(
            jax.ShapeDtypeStruct((total, columns), F32),
            jax.ShapeDtypeStruct(exposures.shape, F32),
        ),
        in_specs=[vmem()] * 2,
        out_specs=(hbm(), hbm()),
        scratch_shapes=[pltpu.SemaphoreType.DMA((8,))],
        compiler_params=pltpu.CompilerParams(vmem_limit_bytes=1024 * 1024),
        name="emit",
    )(updated, residual)
    return updated.reshape(model.shape), residual


def solution(mesh):
    both = ("groups", "sky")
    return jax.shard_map(
        body,
        mesh=mesh,
        in_specs=(
            P(both, None, None, None),
            P(both, None, None),
            P(both),
            P(),
            P(both, None),
            P(both),
            P(both, None),
            P(both, None),
            P(both, None),
            P(both, None),
            P(both, None),
            P(both, None),
            P(both),
            P(both),
        ),
        out_specs=(P(both, None, None, None), P(both, None, None)),
        check_vma=False,
    )
```

```python
import functools

import jax
import jax.numpy as jnp
from jax import lax
from jax.experimental import pallas as pl
from jax.experimental.pallas import tpu as pltpu
from jax.sharding import PartitionSpec as P

NPSF = 4
TAPS = 7
ITERS = 2
F32 = jnp.float32
BF16 = jnp.bfloat16
I32 = jnp.int32


def vmem():
    return pl.BlockSpec(memory_space=pltpu.VMEM)


def hbm():
    return pl.BlockSpec(memory_space=pltpu.HBM)


def round_up(value, multiple):
    return -(-value // multiple) * multiple


def partner(me, i, peers):
    other = 0
    bit = 1
    while bit < peers:
        other = other + lax.rem(lax.div(me, bit) + lax.div(i, bit), 2) * bit
        bit *= 2
    return other


def iota(shape, axis):
    return lax.broadcasted_iota(I32, shape, axis)


def floor_div(value, divisor):
    return jnp.floor((value.astype(F32) + 0.5) * (1.0 / divisor))


def send_table(plane, row, cover, width, tile_rows):
    peers, capacity = plane.shape
    position = iota((peers, width), 1)
    chosen = jnp.zeros((peers, width), I32)
    offset = jnp.zeros((peers, 1), I32)
    for c in range(capacity):
        first = jnp.maximum(plane[:, c : c + 1], 0) * tile_rows + row[:, c : c + 1] - offset
        chosen = jnp.where(position >= offset, first + position, chosen)
        offset = offset + cover[:, c : c + 1]
    return chosen, position < offset


def use_tables(slot, start, stop, peers, capacity, rows_each, width, height):
    meets, count = slot.shape
    which_peer = iota((peers, count), 0).astype(F32)
    exposure = iota((1, count), 1).astype(F32)
    owners, columns, starts, lengths, alive, peer_rows = [], [], [], [], [], []
    for k in range(meets):
        name = slot[k : k + 1, :].astype(F32)
        peer = floor_div(name, capacity)
        owners.append(jnp.where(which_peer == peer, 1.0, 0.0))
        columns.append(name - peer * capacity)
        starts.append(start[k : k + 1, :].astype(F32))
        lengths.append(stop[k : k + 1, :].astype(F32) - starts[k])
        alive.append(name >= 0.0)
        peer_rows.append(peer)
    begin = jnp.zeros((peers, 1), F32)
    found = [jnp.zeros((1, count), F32) for _ in range(meets)]
    position = iota((peers, width), 1).astype(F32)
    chosen = jnp.zeros((peers, width), F32)
    for c in range(capacity):
        length = jnp.zeros((peers, count), F32)
        source = jnp.zeros((peers, count), F32)
        for k in range(meets):
            here = jnp.where(columns[k] == c, owners[k], 0.0)
            length = length + here * lengths[k]
            source = source + here * (exposure * height + starts[k])
            found[k] = found[k] + jnp.sum(here * begin, axis=0, keepdims=True)
        source = jnp.sum(source, axis=1, keepdims=True)
        chosen = jnp.where(position >= begin, source - begin + position, chosen)
        begin = begin + jnp.sum(length, axis=1, keepdims=True)
    give = jnp.clip(chosen.astype(I32), 0, count * height - 1)
    rows = []
    for k in range(meets):
        where = height + peer_rows[k] * rows_each + found[k] - starts[k]
        rows.append(jnp.where(alive[k], where, float(height)))
    for k in range(meets):
        rows.append(jnp.where(alive[k], starts[k], float(height)))
    limits = [peers * rows_each + height] * meets + [height] * meets
    return give, [jnp.clip(value.astype(I32), 0, limit) for value, limit in zip(rows, limits)]


def spread(value, target, direction, masks):
    height, columns = value.shape
    half = TAPS // 2
    for v in range(TAPS):
        shift = direction * (v - half)
        part = value
        if shift != 0:
            part = jnp.where(masks[shift + half], pltpu.roll(value, shift % columns, 1), 0.0)
        target[pl.ds(v * height, height), :] = part.astype(BF16)


def apply(operator, shifted):
    both = jnp.dot(operator, shifted, preferred_element_type=F32)
    height = both.shape[0] // 2
    return both[:height] + both[height:]


def build_operators(taps, expanded, operators, height):
    banks, lanes = taps.shape
    used = 2 * NPSF * TAPS
    group_row = floor_div(iota((lanes, lanes), 0), TAPS)
    group_column = floor_div(iota((lanes, lanes), 1), TAPS)
    lane = iota((lanes, lanes), 1)
    together = jnp.where((group_row == group_column) & (lane < used), 1.0, 0.0)
    raw = taps[...]
    sums = jnp.dot(raw, together, precision=lax.Precision.HIGHEST, preferred_element_type=F32)
    scaled = jnp.where(iota((banks, lanes), 1) < used, raw / jnp.where(sums > 0.0, sums, 1.0), 0.0)
    scaled = scaled.astype(BF16)
    depth = operators.shape[-1]
    tap_of = floor_div(iota((lanes, depth), 1), height).astype(I32)
    column_taps = []
    for j in range(NPSF):
        pick = (iota((lanes, depth), 0) == (NPSF + j) * TAPS + tap_of) & (tap_of < TAPS)
        pick = jnp.where(pick, 1.0, 0.0).astype(BF16)
        column_taps.append(jnp.dot(scaled, pick, preferred_element_type=F32))
    scaled = scaled.astype(F32)
    for u in range(TAPS):
        kernel = jnp.zeros((banks, depth), F32)
        for j in range(NPSF):
            at = j * TAPS + u
            kernel = kernel + scaled[:, at : at + 1] * column_taps[j]
        kernel = kernel * (1.0 / NPSF)
        coarse = kernel.astype(BF16).astype(F32)
        expanded[u, :, :] = coarse
        expanded[TAPS + u, :, :] = kernel - coarse
    lane = iota((height, depth), 1)
    tap = floor_div(lane, height).astype(I32)
    difference = iota((height, depth), 0) - (lane - tap * height)
    inside = tap < TAPS
    half = TAPS // 2

    def one_bank(b, carry):
        for part in range(2):
            ways = [jnp.zeros((height, depth), F32) for _ in range(2)]
            for u in range(TAPS):
                value = expanded[part * TAPS + u, pl.ds(b, 1), :]
                ways[0] = jnp.where(inside & (difference == u - half), value, ways[0])
                ways[1] = jnp.where(inside & (difference == half - u), value, ways[1])
            for way in range(2):
                operators[b, way, pl.ds(part * height, height), :] = ways[way].astype(BF16)
        return carry

    lax.fori_loop(0, banks, one_bank, 0)


def kernel(tile_rows, band_count, unroll, batch_in, weight_in, lo_in, hi_in, step_in, plane_in, row_in, cover_in,
           slot_in, start_in, stop_in, psf_in, exposures, model, updated, residual, batch, weight, lo, hi, step, plane,
           row, cover, slot, start, stop, psf, observed, image, grad, gathered, stamps, forward, backward, rows_out,
           leaving, landing, taps_out, taps_in, taps, expanded, operators, tables, targets, plane_ids, plane_of,
           indices, send_sems, recv_sems, own_sems):
    me = lax.axis_index("sky")
    peers, capacity = plane.shape
    total, columns = image.shape
    count, height, _ = observed.shape
    rows_each = landing.shape[2]
    meets = slot.shape[0]
    width = tables.shape[1]
    own_banks = psf.shape[0]
    half = TAPS // 2
    last = peers - 1

    barrier = pltpu.get_barrier_semaphore()

    def greet(i, carry):
        pl.semaphore_signal(
            barrier, inc=1, device_id={"sky": partner(me, i, peers)}, device_id_type=pl.DeviceIdType.MESH
        )
        return carry

    lax.fori_loop(1, peers, greet, 0)
    pairs = [(plane_in, plane), (row_in, row), (cover_in, cover), (slot_in, slot), (start_in, start), (stop_in, stop),
             (psf_in, psf), (model, image), (batch_in, batch), (weight_in, weight), (lo_in, lo), (hi_in, hi),
             (step_in, step), (exposures, observed)]
    copies = [pltpu.make_async_copy(a, b, own_sems.at[n]) for n, (a, b) in enumerate(pairs)]
    for copy in copies:
        copy.start()
    for copy in copies[:7]:
        copy.wait()

    chosen, used_rows = send_table(plane[...], row[...], cover[...], width, tile_rows)
    tables[pl.ds(0, peers), :] = jnp.clip(chosen, 0, total - 1)
    of_plane = floor_div(chosen, tile_rows)
    plane_ids[...] = of_plane
    targets[...] = jnp.where(used_rows, chosen - of_plane.astype(I32) * tile_rows, -1)
    give, at_rows = use_tables(slot[...], start[...], stop[...], peers, capacity, rows_each, width, height)
    tables[pl.ds(peers, peers), :] = give
    for k, value in enumerate(at_rows):
        tables[pl.ds(2 * peers + k, 1), pl.ds(0, count)] = value
    index_copy = pltpu.make_async_copy(tables, indices, own_sems.at[len(pairs)])
    index_copy.start()

    taps_out[...] = jnp.zeros(taps_out.shape, F32)
    taps_out[pl.ds(0, own_banks), pl.ds(0, psf.shape[1])] = psf[...]
    gathered[pl.ds(0, height), :] = jnp.zeros((height, columns), F32)
    gathered[pl.ds(height + peers * rows_each, height), :] = jnp.zeros((height, columns), F32)
    used = TAPS * height
    spare = forward.shape[1] - used
    if spare:
        for i in range(unroll):
            forward[i, pl.ds(used, spare), :] = jnp.zeros((spare, columns), BF16)
            backward[i, pl.ds(used, spare), :] = jnp.zeros((spare, columns), BF16)
    position = iota((height, columns), 0)
    lane = iota((height, columns), 1)
    masks = [
        (lane >= shift) if shift > 0 else (lane < columns + shift) for shift in range(-half, half + 1)
    ]
    index_copy.wait()
    copies[7].wait()

    def remote(phase, i):
        to = partner(me, i, peers)
        return pltpu.make_async_remote_copy(
            src_ref=leaving.at[phase, to],
            dst_ref=landing.at[phase, me],
            send_sem=send_sems.at[phase, i],
            recv_sem=recv_sems.at[phase, i],
            device_id={"sky": to},
            device_id_type=pl.DeviceIdType.MESH,
        )

    def remote_taps(i):
        return pltpu.make_async_remote_copy(
            src_ref=taps_out,
            dst_ref=taps_in.at[me],
            send_sem=send_sems.at[2 * ITERS, i],
            recv_sem=recv_sems.at[2 * ITERS, i],
            device_id={"sky": partner(me, i, peers)},
            device_id_type=pl.DeviceIdType.MESH,
        )

    def pick_rows(source, table_first, to):
        for p in range(rows_each):
            rows_out[pl.ds(p, 1), :] = source[pl.ds(indices[table_first + to, p], 1), :]
        return rows_out[...].astype(BF16)

    def send_all(phase, source, table_first):
        def one(t, carry):
            i = last - t
            to = partner(me, i, peers)
            leaving[phase, to, :, :] = pick_rows(source, table_first, to)

            @pl.when(t > 0)
            def _():
                remote(phase, i + 1).start()

            return carry

        lax.fori_loop(0, last, one, 0)
        landing[phase, me, :, :] = pick_rows(source, table_first, me)
        remote(phase, 1).start()

    def wait_barrier():
        pl.semaphore_wait(barrier, last)

        def one(t, carry):
            remote_taps(last - t).start()
            return carry

        lax.fori_loop(0, last, one, 0)
        taps_in[me, :, :] = taps_out[...]

    def take_taps():
        def one(t, carry):
            remote_taps(last - t).wait_recv()
            return carry

        lax.fori_loop(0, last, one, 0)

        def place(o, carry):
            taps[pl.ds(o * own_banks, own_banks), :] = taps_in[o, pl.ds(0, own_banks), :]
            return carry

        lax.fori_loop(0, peers, place, 0)
        build_operators(taps, expanded, operators, height)
        for copy in copies[8:]:
            copy.wait()

    quarter = peers // 4 if peers % 4 == 0 else peers

    def arrival(t):
        block = lax.div(t, quarter)
        return (lax.rem(3 * block, 5) - 2 * lax.div(block, 3)) * quarter + lax.rem(t, quarter)

    def take_pieces(phase):
        def one(t, carry):
            i = arrival(t)
            origin = partner(me, i, peers)

            @pl.when(i > 0)
            def _():
                remote(phase, i).wait_recv()

            here = pl.multiple_of(height + origin * rows_each, 8)
            gathered[pl.ds(here, rows_each), :] = landing[phase, origin].astype(F32)
            return carry

        lax.fori_loop(0, peers, one, 0)

    def assemble(e):
        value = None
        for k in range(meets):
            piece = gathered[pl.ds(indices[2 * peers + k, e], height), :]
            first = indices[2 * peers + meets + k, e]
            value = piece if value is None else jnp.where(position >= first, piece, value)
        return value

    def deblend():
        def group(g, carry):
            which = [g * unroll + i for i in range(unroll)]
            for i, e in enumerate(which):
                spread(assemble(e), forward.at[i], 1, masks)
            for i, e in enumerate(which):
                predicted = apply(operators[batch[e], 0], forward[i])
                error = weight[e] * (predicted - observed[e].astype(F32))
                residual[e] = error
                spread(error, backward.at[i], -1, masks)
            for i, e in enumerate(which):
                here = pl.multiple_of(e * height, 8)
                stamps[pl.ds(here, height), :] = apply(operators[batch[e], 1], backward[i])
            return carry

        lax.fori_loop(0, count // unroll, group, 0)

    together = 4 if rows_each % 128 == 0 and peers % 4 == 0 else 1
    planes = total // tile_rows
    wide = 2 if planes % 2 == 0 else 1

    def spread_planes():
        eye = iota((rows_each, width), 0) == iota((rows_each, width), 1)

        def one(o, carry):
            ids = jnp.where(eye, plane_ids[pl.ds(o, 1), :], 0.0)
            ids = jnp.sum(ids, axis=1, keepdims=True)
            plane_of[o, :, :] = jnp.broadcast_to(ids, (rows_each, columns)).astype(BF16)
            return carry

        lax.fori_loop(0, peers, one, 0)

    def clear():
        def one(p, carry):
            grad[p, :, :] = jnp.zeros((tile_rows, columns), F32)
            return carry

        lax.fori_loop(0, planes, one, 0)

    def joined(values, axis):
        return values[0] if len(values) == 1 else jnp.concatenate(values, axis=axis)

    def add_returned(phase):
        def one(q, carry):
            names, parts, owners = [], [], []
            for j in range(together):
                i = arrival(q * together + j)
                origin = partner(me, i, peers)

                @pl.when(i > 0)
                def _():
                    remote(phase, i).wait_recv()

                names.append(targets[pl.ds(origin, 1), :][:, :rows_each])
                parts.append(landing[phase, origin])
                owners.append(plane_of[origin])
            name, part, owner = joined(names, 1), joined(parts, 0), joined(owners, 0)
            hit = iota((tile_rows, name.shape[1]), 0) == name
            chosen = jnp.where(hit, 1.0, 0.0).astype(BF16)
            for p in range(0, planes, wide):
                mine = [jnp.where(owner == float(p + w), part, jnp.zeros_like(part)) for w in range(wide)]
                both = jnp.dot(chosen, joined(mine, 1), preferred_element_type=F32)
                for w in range(wide):
                    grad[p + w, :, :] += both[:, w * columns : (w + 1) * columns]
            return carry

        lax.fori_loop(0, peers // together, one, 0)

    tile_position = iota((tile_rows, columns), 0)

    def move(target):
        def one_plane(p, carry):
            tile = lax.div(p, band_count)
            here = pl.ds(pl.multiple_of(p * tile_rows, 8), tile_rows)
            moved = jnp.maximum(image[here, :] - step[lax.rem(p, band_count)] * grad[p], 0.0)
            moved = jnp.where((tile_position >= lo[tile]) & (tile_position < hi[tile]), moved, 0.0)
            target[here, :] = moved
            return carry

        lax.fori_loop(0, total // tile_rows, one_plane, 0)

    wait_barrier()
    for sweep in range(ITERS):
        send_all(2 * sweep, image, 0)
        if sweep == 0:
            spread_planes()
            take_taps()
        take_pieces(2 * sweep)
        deblend()
        send_all(2 * sweep + 1, stamps, peers)
        clear()
        add_returned(2 * sweep + 1)
        move(updated if sweep == ITERS - 1 else image)

    def drain(t, carry):
        for phase in range(2 * ITERS):
            remote(phase, last - t).wait_send()
        remote_taps(last - t).wait_send()
        return carry

    lax.fori_loop(0, last, drain, 0)


def emit_kernel(updated, residual, updated_out, residual_out, sems):
    copies = []
    for source, target in ((updated, updated_out), (residual, residual_out)):
        rows = source.shape[0] // 4
        for n in range(4):
            part = pl.ds(n * rows, rows)
            copies.append(pltpu.make_async_copy(source.at[part], target.at[part], sems.at[len(copies)]))
            copies[-1].start()
    for copy in copies:
        copy.wait()


def body(model, exposures, inv_var, step_size, psf_taps, exp_batch, send_plane, send_row, send_cover, use_slot,
         use_start, use_stop, foot_lo, foot_hi):
    tile_count, band_count, tile_rows, columns = model.shape
    count, height, _ = exposures.shape
    peers, capacity = send_plane.shape
    meets = use_slot.shape[1]
    rows_each = capacity * height // 2
    total = tile_count * band_count * tile_rows
    packed_rows = peers * rows_each
    own_banks = psf_taps.shape[0]
    tap_rows = round_up(own_banks, 8)
    depth = round_up(TAPS * height, 128)
    unroll = count
    width = round_up(max(rows_each, count), 128)
    table_rows = 2 * peers + round_up(2 * meets, 8)
    banks = peers * own_banks
    operands = (exp_batch, inv_var, foot_lo, foot_hi, step_size, send_plane, send_row, send_cover, use_slot.T,
                use_start.T, use_stop.T, psf_taps, exposures, model.reshape(total, columns))
    updated, residual = pl.pallas_call(
        functools.partial(kernel, tile_rows, band_count, unroll),
        out_shape=(
            jax.ShapeDtypeStruct((total, columns), F32),
            jax.ShapeDtypeStruct(exposures.shape, F32),
        ),
        in_specs=[hbm()] * len(operands),
        out_specs=(vmem(), vmem()),
        scratch_shapes=[pltpu.SMEM(value.shape, value.dtype) for value in operands[:5]]
        + [pltpu.VMEM(value.shape, value.dtype) for value in operands[5:]]
        + [
            pltpu.VMEM((tile_count * band_count, tile_rows, columns), F32),
            pltpu.VMEM((packed_rows + 2 * height, columns), F32),
            pltpu.VMEM((count * height, columns), F32),
            pltpu.VMEM((unroll, depth, columns), BF16),
            pltpu.VMEM((unroll, depth, columns), BF16),
            pltpu.VMEM((rows_each, columns), F32),
            pltpu.VMEM((2 * ITERS, peers, rows_each, columns), BF16),
            pltpu.VMEM((2 * ITERS, peers, rows_each, columns), BF16),
            pltpu.VMEM((tap_rows, 128), F32),
            pltpu.VMEM((peers, tap_rows, 128), F32),
            pltpu.VMEM((banks, 128), F32),
            pltpu.VMEM((2 * TAPS, banks, depth), F32),
            pltpu.VMEM((banks, 2, 2 * height, depth), BF16),
            pltpu.VMEM((table_rows, width), I32),
            pltpu.VMEM((peers, width), I32),
            pltpu.VMEM((peers, width), F32),
            pltpu.VMEM((peers, rows_each, columns), BF16),
            pltpu.SMEM((table_rows, width), I32),
            pltpu.SemaphoreType.DMA((2 * ITERS + 1, peers)),
            pltpu.SemaphoreType.DMA((2 * ITERS + 1, peers)),
            pltpu.SemaphoreType.DMA((len(operands) + 1,)),
        ],
        compiler_params=pltpu.CompilerParams(
            collective_id=0, has_side_effects=True, vmem_limit_bytes=40 * 1024 * 1024
        ),
        name="deblend",
    )(*[pltpu.with_memory_space_constraint(value, pltpu.HBM) for value in operands])
    updated, residual = pl.pallas_call(
        emit_kernel,
        out_shape=(
            jax.ShapeDtypeStruct((total, columns), F32),
            jax.ShapeDtypeStruct(exposures.shape, F32),
        ),
        in_specs=[vmem()] * 2,
        out_specs=(hbm(), hbm()),
        scratch_shapes=[pltpu.SemaphoreType.DMA((8,))],
        compiler_params=pltpu.CompilerParams(vmem_limit_bytes=1024 * 1024),
        name="emit",
    )(updated, residual)
    return updated.reshape(model.shape), residual


def solution(mesh):
    both = ("groups", "sky")
    return jax.shard_map(
        body,
        mesh=mesh,
        in_specs=(
            P(both, None, None, None),
            P(both, None, None),
            P(both),
            P(),
            P(both, None),
            P(both),
            P(both, None),
            P(both, None),
            P(both, None),
            P(both, None),
            P(both, None),
            P(both, None),
            P(both),
            P(both),
        ),
        out_specs=(P(both, None, None, None), P(both, None, None)),
        check_vma=False,
    )
```
